32 devices in a mesh: seq: 8 (over z, y), head: 4 (over x, core).
Axes of the slice: x: 2, y: 2, z: 4, core: 2. Of those that a mesh axis runs over, the one named last changes fastest.
Arguments:
- queries: bfloat16 [3072, 2048], P('seq', 'head'), may hold values from -6 to 6
- keys: bfloat16 [3072, 2048], P('seq', 'head'), may hold values from -6 to 6
- values: bfloat16 [3072, 2048], P('seq', 'head'), may hold values from -6 to 6
- grad_out: bfloat16 [3072, 2048], P('seq', 'head'), may hold values from -6 to 6
- anchor_ids: int32 [24, 32], P('seq'), may hold values from 0 to 3071, as said below
- link_counts: int32 [24], P('seq'), may hold values from 24 to 32
- doc_lengths: int32 [6], replicated, may hold values from 1 to 1536, 3072 in all
Outputs:
- grad_queries: bfloat16 [3072, 2048], P('seq', 'head')
- grad_keys: bfloat16 [3072, 2048], P('seq', 'head')
- grad_values: bfloat16 [3072, 2048], P('seq', 'head')
The draws below stay inside these ranges and needn't reach their ends.
Inputs may be any that keep to these rules, and one draw needn't show every extreme that they name: `anchor_ids`: entry j of block b is used only for j < link_counts[b]. Over the live entries of the 3 blocks of one index of seq, the tokens named are distinct, and at most 48 of them lie among the 384 tokens of any one index of seq; in every draw that bound is reached, and some index of seq receives 48 live links from every index of seq. `doc_lengths`: the lengths sum to 3072.
All inputs are finite; a program needn't handle non-finite values.
Results may differ from the reference program's by a relative error of at most 0.011.
Values may be sent and summed in bfloat16 or wider, within the bound.
A program may use at most 64 MiB of HBM per device.

```python
import math
import jax
import jax.numpy as jnp
import numpy as np
from jax import lax

D = 2048
HEADS = 16
HD = 128
BLK = 128
LINKS = 32
BLK_DEV = 3
TOK_DEV = 384
TOKENS = 3072
NBLK = 24
CAP = 48
NDOCS = 6
DOC_MOST = 1536
N_SEQ = 8


def draw_queries(key, part):
    drawn_key = jax.random.fold_in(key, 1)
    drawn = jnp.clip(jax.random.normal(drawn_key, (TOKENS, D), jnp.float32), -6.0, 6.0)
    return drawn.astype(jnp.bfloat16)


def draw_keys(key, part):
    drawn_key = jax.random.fold_in(key, 2)
    drawn = jnp.clip(jax.random.normal(drawn_key, (TOKENS, D), jnp.float32), -6.0, 6.0)
    return drawn.astype(jnp.bfloat16)


def link_plan(key):
    base = jax.random.fold_in(key, 23)
    split_keys = jax.random.split(base, 6)
    group_count = N_SEQ // 4
    owning_index = jnp.arange(N_SEQ, dtype=jnp.int32)
    busiest_anchor = jax.random.randint(split_keys[0], (), 0, N_SEQ)
    warm_set = jax.random.randint(split_keys[1], (4,), 0, N_SEQ)
    random_perturbation = jax.random.randint(split_keys[2], (N_SEQ, N_SEQ), 0, 1024)
    warm_flag = jnp.any(owning_index[:, None] == warm_set[None, :], axis=1)
    extra_reward = jnp.where(owning_index == busiest_anchor, 4096, jnp.where(warm_flag, 1024, 0))
    popularity_order = (random_perturbation + extra_reward[None, :]) * N_SEQ + owning_index[None, :]
    _, picked = lax.top_k(popularity_order, group_count)
    slot_count = BLK_DEV * LINKS
    slot_index = jnp.arange(slot_count, dtype=jnp.int32)
    group_of = slot_index // CAP
    within = slot_index % CAP
    owner_dev = picked[:, group_of]
    stride = TOK_DEV // CAP
    group_start = jax.random.randint(split_keys[3], (N_SEQ, group_count), 0, TOK_DEV)
    jitter = jax.random.randint(split_keys[4], (N_SEQ, slot_count), 0, stride)
    position = (group_start[:, group_of] + within * stride + jitter) % TOK_DEV
    link_ids = (owner_dev * TOK_DEV + position).reshape(NBLK, LINKS).astype(jnp.int32)
    local_block = jnp.arange(NBLK, dtype=jnp.int32) % BLK_DEV
    counts = jax.random.randint(split_keys[5], (NBLK,), LINKS * 3 // 4, LINKS + 1)
    counts = jnp.where(local_block * LINKS < CAP, LINKS, counts).astype(jnp.int32)
    return (link_ids, counts)


def draw_anchor_ids(key, part):
    link_ids, counts = link_plan(key)
    return link_ids


def draw_link_counts(key, part):
    link_ids, counts = link_plan(key)
    return counts


def block_scale(stream_key, shape, shards, smallest, top_value):
    def one(axis_at, shards_of):
        steps = jax.random.uniform(jax.random.fold_in(jax.random.fold_in(stream_key, 6), axis_at), (shards_of,), jnp.float32, smallest / len(shards), top_value / len(shards))
        return jnp.repeat(jnp.exp(steps), shape[axis_at] // shards_of).reshape((-1,) + (1,) * (len(shape) - axis_at - 1))

    loudness = one(*shards[0])
    for cut in shards[1:]:
        loudness = loudness * one(*cut)
    return loudness


def length_profile(count, total, bound, lean):
    loads = [(1 << 20) // math.isqrt(grade ** lean) + 1 for grade in range(2, count + 1)]
    surplus, given = total - bound - (count - 1), [1] * (count - 1)
    while surplus > 0:
        movable = [i for i in range(count - 1) if given[i] < bound]
        pool, remaining = sum([loads[i] for i in movable]), surplus
        for i in movable:
            extra = min(bound - given[i], max(1, remaining * loads[i] // pool), surplus)
            given[i] = given[i] + extra
            surplus = surplus - extra
    return np.array([bound] + given)


def uneven(own_key, amount, total, reach, skew):
    if amount == 2:
        one = jax.random.randint(own_key, (), max(1, total - reach), min(reach, total - 1) + 1)
        return jnp.stack([one, total - one])
    tallies = jnp.asarray(length_profile(amount, total, reach, skew), jnp.int32)
    twos = (amount - 1) // 2
    giver, taker = tallies[1:1 + 2 * twos:2], tallies[2:2 + 2 * twos:2]
    margin = jnp.minimum(giver - 1, reach - taker)
    shifted = jax.random.randint(jax.random.fold_in(own_key, 1), (twos,), 0, 1 << 20) % (margin + 1)
    tallies = tallies.at[1:1 + 2 * twos:2].set(giver - shifted).at[2:2 + 2 * twos:2].set(taker + shifted)
    return tallies[jax.random.permutation(jax.random.fold_in(own_key, 2), amount)]


def centred(key, dims, scale, reach, shards=(), kind=jnp.bfloat16):
    entries = jax.random.normal(key, dims, jnp.float32) * scale
    if len(shards) > 0:
        entries = block_scale(key, dims, shards, -0.22, 0.18) * entries
    return jnp.clip(entries, min=-reach, max=reach).astype(kind)


def setup_inputs(seed: int = 0) -> dict:
    seeds = jax.random.split(jax.random.key(seed), 8)
    return {
        "queries": draw_queries(jax.random.fold_in(seeds[7], 71), 0),
        "keys": draw_keys(jax.random.fold_in(seeds[7], 71), 0),
        "values": centred(seeds[2], (TOKENS, D), 1.0, 6.0, ((0, 8), (1, 4))),
        "grad_out": centred(seeds[3], (TOKENS, D), 1.0, 6.0, ((0, 8), (1, 4))),
        "anchor_ids": draw_anchor_ids(jax.random.fold_in(seeds[7], 71), 0),
        "link_counts": draw_link_counts(jax.random.fold_in(seeds[7], 71), 0),
        "doc_lengths": uneven(seeds[6], NDOCS, TOKENS, DOC_MOST, 2).astype(jnp.int32),
    }


def document_index(doc_lengths, positions):
    doc_starts = jnp.cumsum(doc_lengths) - doc_lengths
    found = jnp.sum((doc_starts[None, :] <= positions[:, None]).astype(jnp.int32), axis=1) - 1
    inside = (positions >= 0) & (positions < TOKENS)
    return jnp.where(inside, found, -1).astype(jnp.int32)


def reference(queries, keys, values, grad_out, anchor_ids, link_counts, doc_lengths):
    score_scale = float(HD) ** -0.5
    rim_rows = 2 * BLK
    window_keys = 5 * BLK
    positions = jnp.arange(TOKENS + 2 * rim_rows, dtype=jnp.int32) - rim_rows
    doc_ext = document_index(doc_lengths, positions)
    zero_rim = jnp.zeros((rim_rows, D), jnp.bfloat16)
    key_pad = jnp.concatenate([zero_rim, keys, zero_rim], axis=0)
    value_pad = jnp.concatenate([zero_rim, values, zero_rim], axis=0)
    slot_index = jnp.arange(LINKS, dtype=jnp.int32)

    def one_block(carry, block):
        grad_key_acc, grad_value_acc = carry
        start = (block * BLK).astype(jnp.int32)
        query_blk = lax.dynamic_slice_in_dim(queries, start, BLK, 0).astype(jnp.float32).reshape(BLK, HEADS, HD)
        grad_blk = lax.dynamic_slice_in_dim(grad_out, start, BLK, 0).astype(jnp.float32).reshape(BLK, HEADS, HD)
        key_win = lax.dynamic_slice_in_dim(key_pad, start, window_keys, 0)
        value_win = lax.dynamic_slice_in_dim(value_pad, start, window_keys, 0)
        doc_query = lax.dynamic_slice_in_dim(doc_ext, start + rim_rows, BLK, 0)
        doc_win = lax.dynamic_slice_in_dim(doc_ext, start, window_keys, 0)
        link_ids = anchor_ids[block]
        is_live = slot_index < link_counts[block]
        key_all = jnp.concatenate([key_win, keys[link_ids]], axis=0).astype(jnp.float32).reshape(-1, HEADS, HD)
        value_all = jnp.concatenate([value_win, values[link_ids]], axis=0).astype(jnp.float32).reshape(-1, HEADS, HD)
        allowed = jnp.concatenate([doc_query[:, None] == doc_win[None, :], jnp.broadcast_to(is_live[None, :], (BLK, LINKS))], axis=1)[None]
        scores = jnp.einsum("qhd,khd->hqk", query_blk, key_all) * score_scale
        row_max = jnp.max(jnp.where(allowed, scores, -1e30), axis=-1, keepdims=True)
        expd = jnp.where(allowed, jnp.exp(scores - row_max), 0.0)
        weights = expd / jnp.sum(expd, axis=-1, keepdims=True)
        weights_b = lax.optimization_barrier(weights.astype(jnp.bfloat16)).astype(jnp.float32)
        output = jnp.einsum("hqk,khd->qhd", weights_b, value_all)
        row_delta = jnp.sum(grad_blk * output, axis=-1)
        grad_weights = jnp.einsum("qhd,khd->hqk", grad_blk, value_all)
        grad_scores = weights * (grad_weights - jnp.transpose(row_delta)[:, :, None])
        grad_scores_b = lax.optimization_barrier(grad_scores.astype(jnp.bfloat16)).astype(jnp.float32)
        grad_query = (jnp.einsum("hqk,khd->qhd", grad_scores_b, key_all) * score_scale).reshape(BLK, D).astype(jnp.bfloat16)
        grad_key = (jnp.einsum("hqk,qhd->khd", grad_scores_b, query_blk) * score_scale).reshape(-1, D)
        grad_value = jnp.einsum("hqk,qhd->khd", weights_b, grad_blk).reshape(-1, D)
        window_k = lax.dynamic_slice_in_dim(grad_key_acc, start, window_keys, 0) + grad_key[:window_keys]
        window_v = lax.dynamic_slice_in_dim(grad_value_acc, start, window_keys, 0) + grad_value[:window_keys]
        grad_key_acc = lax.dynamic_update_slice_in_dim(grad_key_acc, window_k, start, 0)
        grad_value_acc = lax.dynamic_update_slice_in_dim(grad_value_acc, window_v, start, 0)
        grad_key_acc = grad_key_acc.at[link_ids + rim_rows].add(grad_key[window_keys:])
        grad_value_acc = grad_value_acc.at[link_ids + rim_rows].add(grad_value[window_keys:])
        return (grad_key_acc, grad_value_acc), grad_query

    initial = (jnp.zeros((TOKENS + 2 * rim_rows, D), jnp.float32), jnp.zeros((TOKENS + 2 * rim_rows, D), jnp.float32))
    (grad_key_acc, grad_value_acc), grad_query = lax.scan(one_block, initial, jnp.arange(NBLK, dtype=jnp.int32))
    grad_queries = grad_query.reshape(TOKENS, D)
    grad_keys = grad_key_acc[rim_rows:rim_rows + TOKENS].astype(jnp.bfloat16)
    grad_values = grad_value_acc[rim_rows:rim_rows + TOKENS].astype(jnp.bfloat16)
    return (grad_queries, grad_keys, grad_values)
```

```python
import functools

import jax
import jax.numpy as jnp
from jax import lax
from jax.experimental import pallas as pl
from jax.experimental.pallas import tpu as pltpu
from jax.sharding import PartitionSpec as P

HD = 128
BLK = 128
LINKS = 32
RIM = 2 * BLK
CHUNKS = 4
WIN = 5 * BLK
MESH = pl.DeviceIdType.MESH
F32 = jnp.float32
BF16 = jnp.bfloat16


def dot(a, b, ca, cb):
    return lax.dot_general(a, b, (((ca,), (cb,)), ((), ())), preferred_element_type=F32)


def body(
    n, cap, ndocs,
    q_hbm, k_ref, v_ref, go_hbm, ids_hbm, cnt_ref, len_ref,
    gq_ref, gk_ref, gv_ref,
    q_ref, go_ref, ids_s, meta_ref, l_ss,
    kx, vx, meta_all, rank_s, sel, own_hot, sendbuf, arr, ak, av,
    acck, accv, anck, ancv, gsend, ginc, far_out, far_in, near_out, near_in, bias_s,
    meta_ss, meta_rs, m_ss, m_rs, r_ss, r_rs, a_ss, a_rs, g_ss, g_rs, f_ss, f_rs, b_ss, b_rs,
):
    rows, cols = q_hbm.shape
    heads = cols // HD
    blocks = rows // BLK
    chunks = CHUNKS
    width = cols // chunks
    scale = float(HD) ** (-0.5)
    me = lax.axis_index("seq")
    unroll = n <= 8

    def loop(lo, hi, f):
        def g(i, c):
            f(i)
            return c
        lax.fori_loop(lo, hi, g, 0, unroll=unroll)

    def peer(i):
        return lax.rem(me + i, n)

    def at(ref, d):
        return ref.at[pl.ds(pl.multiple_of(d * cap, cap), cap)]

    def rcopy(src, dst, ss, rs, d):
        return pltpu.make_async_remote_copy(
            src_ref=src, dst_ref=dst, send_sem=ss, recv_sem=rs,
            device_id={"seq": d}, device_id_type=MESH,
        )

    barrier = pltpu.get_barrier_semaphore()
    loop(1, n, lambda i: pl.semaphore_signal(
        barrier, inc=1, device_id={"seq": peer(i)}, device_id_type=MESH))

    home = [
        pltpu.make_async_copy(src, dst, l_ss.at[i])
        for i, (src, dst) in enumerate((
            (ids_hbm, ids_s),
            (k_ref, kx.at[pl.ds(rows, rows)]),
            (v_ref, vx.at[pl.ds(rows, rows)]),
            (q_hbm, q_ref),
            (go_hbm, go_ref),
        ))
    ]
    for copy in home:
        copy.start()

    lane_a = lax.broadcasted_iota(jnp.int32, (128, 128), 0)
    lane_b = lax.broadcasted_iota(jnp.int32, (128, 128), 1)
    upper = (lane_a < lane_b).astype(BF16)
    home[0].wait()
    slot_lane = lax.broadcasted_iota(jnp.int32, (8, 128), 1)
    ids = jnp.full((8, 128), -1, jnp.int32)
    for b in range(blocks):
        listed = jnp.concatenate(
            [ids_s[b:b + 1], jnp.full((1, 128 - LINKS), -1, jnp.int32)], axis=1)
        moved = pltpu.roll(jnp.broadcast_to(listed, (8, 128)), b * LINKS, 1) if b else jnp.broadcast_to(listed, (8, 128))
        first_lane = b * LINKS
        ids = jnp.where((slot_lane >= first_lane) & (slot_lane < first_lane + cnt_ref[b]), moved, ids)
    meta_ref[...] = ids
    slot = lax.broadcasted_iota(jnp.int32, (cap, 128), 0)

    def hot(inside, rank):
        return jnp.where(
            (rank[0:1].astype(jnp.int32) == slot) & (inside[0:1] > 0.5), 1.0, 0.0
        ).astype(BF16)

    def inside_of(values, owner):
        return jnp.where((values >= owner * rows) & (values < (owner + 1) * rows), 1.0, 0.0)

    pl.semaphore_wait(barrier, n - 1)

    loop(1, n, lambda i: rcopy(
        meta_ref, meta_all.at[me], meta_ss.at[peer(i)], meta_rs.at[me], peer(i)).start())

    par = lax.rem(me, 2)
    mate = me + 1 - 2 * par

    def span(start, length):
        return pl.ds(pl.multiple_of(start, BLK), length)

    def pick(even, odd):
        return even + par * (odd - even)

    def chunk_cols(c):
        return pl.ds(c * width, width)

    kv = ((k_ref, kx), (v_ref, vx))

    def to_mate(c, part):
        start = pick(0, BLK) if part == 0 else pick(RIM, 0)
        length = RIM if part == 0 else BLK
        goal = pick(0, 2 * rows) + start
        return [
            rcopy(src.at[span(start, length), chunk_cols(c)],
                  dst.at[span(goal, length), chunk_cols(c)],
                  m_ss.at[4 * c + 2 * part + t], m_rs.at[4 * c + 2 * part + t], mate)
            for t, (src, dst) in enumerate(kv)
        ]

    ahead = jnp.clip(pick(me + 2, me - 2), 0, n - 1)
    behind = jnp.clip(pick(me - 2, me + 2), 0, n - 1)
    has_ahead = (pick(me + 2, me - 2) >= 0) & (pick(me + 2, me - 2) < n)
    has_behind = (pick(me - 2, me + 2) >= 0) & (pick(me - 2, me + 2) < n)

    def relay(c):
        return [
            rcopy(x.at[span(pick(2 * rows + BLK, 0), RIM), chunk_cols(c)],
                  x.at[span(pick(BLK, 2 * rows), RIM), chunk_cols(c)],
                  r_ss.at[2 * c + t], r_rs.at[2 * c + t], ahead)
            for t, x in enumerate((kx, vx))
        ]

    for c in range(chunks):
        for copy in to_mate(c, 0):
            copy.start()

    meta_all[me] = ids

    @pl.when(jnp.logical_not(has_behind))
    def _():
        kx[span(pick(BLK, 2 * rows), RIM)] = jnp.zeros((RIM, cols), BF16)
        vx[span(pick(BLK, 2 * rows), RIM)] = jnp.zeros((RIM, cols), BF16)

    acck[...] = jnp.zeros_like(acck)
    accv[...] = jnp.zeros_like(accv)
    anck[...] = jnp.zeros_like(anck)
    ancv[...] = jnp.zeros_like(ancv)

    def own_one(o):
        inside = inside_of(ids, o)
        at(own_hot, o)[...] = hot(inside, dot(inside.astype(BF16), upper, 1, 0))

    loop(0, n, own_one)

    base = me * rows - RIM
    pos_l = base + lax.broadcasted_iota(jnp.int32, (8, rows + 2 * RIM), 1)
    pos_s = me * rows + lax.broadcasted_iota(jnp.int32, (rows, 128), 0)

    def count(k, c):
        start, dl, ds = c
        return (
            start + len_ref[k],
            dl + jnp.where(start <= pos_l, 1, 0),
            ds + jnp.where(start <= pos_s, 1, 0),
        )

    _, doc_l, doc_s = lax.fori_loop(
        0, ndocs, count,
        (jnp.int32(0), jnp.full(pos_l.shape, -1, jnp.int32), jnp.full(pos_s.shape, -1, jnp.int32)),
        unroll=ndocs <= 8,
    )
    doc_l = jnp.where((pos_l >= 0) & (pos_l < n * rows), doc_l, -1)

    def meta_wait(i):
        s = peer(i)
        rcopy(meta_ref, meta_all.at[s], meta_ss.at[s], meta_rs.at[s], s).wait()

    loop(1, n, meta_wait)
    row_id = me * rows + lax.broadcasted_iota(jnp.int32, (rows, 128), 0)
    every = meta_all[...].reshape(n * 8, 128)
    rank_s[...] = dot(inside_of(every, me).astype(BF16), upper, 1, 0).reshape(n, 8, 128)

    def sel_one(d):
        theirs = meta_all[d]
        oh = hot(inside_of(theirs, me), rank_s[d])
        place = jnp.where(theirs[0:1] == row_id, 1.0, 0.0).astype(BF16)
        at(sel, d)[...] = dot(oh, place, 1, 1).astype(BF16)

    loop(0, n, sel_one)
    def a_copy(c, d, slot_of):
        return rcopy(at(sendbuf.at[c], d), at(arr.at[c], slot_of),
                     a_ss.at[c, d], a_rs.at[c, slot_of], d)

    for copy in home[1:]:
        copy.wait()
    for c in range(chunks):
        cs = slice(c * width, (c + 1) * width)
        sendbuf[c, :, :width] = dot(sel[...], kx[rows:2 * rows, cs], 1, 0).astype(BF16)
        sendbuf[c, :, width:] = dot(sel[...], vx[rows:2 * rows, cs], 1, 0).astype(BF16)
        at(arr.at[c], me)[...] = at(sendbuf.at[c], me)[...]
    for c in range(chunks):
        for copy in to_mate(c, 0):
            copy.wait()

        @pl.when(has_ahead)
        def _():
            for copy in relay(c):
                copy.start()

        loop(1, n, lambda i: a_copy(c, peer(i), me).start())
        for copy in to_mate(c, 1):
            copy.start()

    lanes = lax.broadcasted_iota(jnp.int32, (BLK, 128), 1)
    live = jnp.broadcast_to(ids[0:1], (BLK, 128)) >= 0
    for b in range(blocks):
        r0 = b * BLK
        same = doc_s[r0:r0 + BLK, 0:1] == doc_l[0:1, r0:r0 + WIN]
        linked = live & (lanes >= b * LINKS) & (lanes < (b + 1) * LINKS)
        bias_s[b] = jnp.concatenate(
            [jnp.where(same, 0.0, -1e30), jnp.where(linked, 0.0, -1e30)], axis=1)

    first = rows - RIM

    def far_copy(c):
        return rcopy(far_out.at[c], far_in.at[c], f_ss.at[c], f_rs.at[c], behind)

    def near_copy(c, part):
        length = BLK if part == 0 else RIM
        start = pick(0, RIM) if part == 0 else pick(BLK, 0)
        return rcopy(near_out.at[c, span(start, length)], near_in.at[c, span(start, length)],
                     b_ss.at[2 * c + part], b_rs.at[2 * c + part], mate)

    def g_copy(c, d, slot_of):
        return rcopy(at(gsend.at[c], d), at(ginc.at[c], slot_of),
                     g_ss.at[c, d], g_rs.at[c, slot_of], d)

    for c in range(chunks):
        cs = slice(c * width, (c + 1) * width)
        for copy in to_mate(c, 1):
            copy.wait()

        @pl.when(has_ahead)
        def _():
            for copy in relay(c):
                copy.wait_send()

        @pl.when(has_behind)
        def _():
            for copy in relay(c):
                copy.wait_recv()

        loop(1, n, lambda i: a_copy(c, peer(i), peer(i)).wait())
        got = dot(own_hot[...], arr[c], 0, 0).astype(BF16)
        ak[:, cs] = got[:, :width]
        av[:, cs] = got[:, width:]
        for b in range(blocks):
            r0 = b * BLK
            w0 = first + r0

            def one_head(h, carry):
                col = pl.ds(pl.multiple_of(c * width + h * HD, HD), HD)
                qb = q_ref[r0:r0 + BLK, col]
                gb = go_ref[r0:r0 + BLK, col]
                kw = jnp.concatenate([kx[w0:w0 + WIN, col], ak[:, col]], axis=0)
                vw = jnp.concatenate([vx[w0:w0 + WIN, col], av[:, col]], axis=0)
                allowed = bias_s[b] == 0.0
                s = jnp.where(allowed, dot(qb, kw, 1, 1) * scale, -1e30)
                top = jnp.max(s, axis=1, keepdims=True)
                e = jnp.where(allowed, jnp.exp(s - top), 0.0)
                w = e / jnp.sum(e, axis=1, keepdims=True)
                wb = w.astype(BF16)
                gw = dot(gb, vw, 1, 1)
                delta = jnp.sum(wb.astype(F32) * gw, axis=1, keepdims=True)
                ds = (w * (gw - delta)).astype(BF16)
                gq_ref[r0:r0 + BLK, col] = (dot(ds, kw, 1, 0) * scale).astype(BF16)
                dk = dot(ds, qb, 0, 0) * scale
                dv = dot(wb, gb, 0, 0)
                acck[w0:w0 + WIN, col] += dk[:WIN]
                accv[w0:w0 + WIN, col] += dv[:WIN]
                anck[:, col] += dk[WIN:]
                ancv[:, col] += dv[WIN:]
                return carry

            lax.fori_loop(0, width // HD, one_head, 0, unroll=True)

        far = span(pick(BLK, 2 * rows), RIM)
        far_out[c, :, :width] = acck[far, cs].astype(BF16)
        far_out[c, :, width:] = accv[far, cs].astype(BF16)
        near = span(pick(2 * rows, RIM), BLK)
        near_out[c, span(pick(0, RIM), BLK), :width] = acck[near, cs].astype(BF16)
        near_out[c, span(pick(0, RIM), BLK), width:] = accv[near, cs].astype(BF16)

        @pl.when(has_behind)
        def _():
            far_copy(c).start()

        near_copy(c, 0).start()
        gsend[c, :, :width] = dot(own_hot[...], anck[:, cs].astype(BF16), 1, 0).astype(BF16)
        gsend[c, :, width:] = dot(own_hot[...], ancv[:, cs].astype(BF16), 1, 0).astype(BF16)
        loop(1, n, lambda i: g_copy(c, peer(i), me).start())
        at(ginc.at[c], me)[...] = at(gsend.at[c], me)[...]

    for c in range(chunks):
        cs = slice(c * width, (c + 1) * width)
        mine = span(pick(2 * rows + BLK, 0), RIM)

        @pl.when(has_behind)
        def _():
            far_copy(c).wait_send()

        @pl.when(has_ahead)
        def _():
            far_copy(c).wait_recv()
            acck[mine, cs] += far_in[c, :, :width].astype(F32)
            accv[mine, cs] += far_in[c, :, width:].astype(F32)

        near_out[c, span(pick(BLK, 0), RIM), :width] = acck[mine, cs].astype(BF16)
        near_out[c, span(pick(BLK, 0), RIM), width:] = accv[mine, cs].astype(BF16)
        near_copy(c, 1).start()

    for c in range(chunks):
        cs = slice(c * width, (c + 1) * width)
        loop(1, n, lambda i: g_copy(c, peer(i), peer(i)).wait())
        acck[rows:2 * rows, cs] += dot(sel[...], ginc[c, :, :width], 0, 0)
        accv[rows:2 * rows, cs] += dot(sel[...], ginc[c, :, width:], 0, 0)

    for c in range(chunks):
        cs = slice(c * width, (c + 1) * width)
        for part in range(2):
            near_copy(c, part).wait_send()
            near_copy(c, part).wait_recv()
        gk_ref[:, cs] = (acck[rows:2 * rows, cs] + near_in[c, :, :width].astype(F32)).astype(BF16)
        gv_ref[:, cs] = (accv[rows:2 * rows, cs] + near_in[c, :, width:].astype(F32)).astype(BF16)


def emit(gq, gk, gv, oq, ok, ov, sems):
    copies = [
        pltpu.make_async_copy(src, dst, sems.at[i])
        for i, (src, dst) in enumerate(((gq, oq), (gk, ok), (gv, ov)))
    ]
    for copy in copies:
        copy.start()
    for copy in copies:
        copy.wait()


def on_device(queries, keys, values, grad_out, anchor_ids, link_counts, doc_lengths):
    rows, cols = queries.shape
    blocks = rows // BLK
    n = lax.axis_size("seq")
    cap = -(-(4 * blocks * LINKS // n) // 16) * 16
    vmem = pl.BlockSpec(memory_space=pltpu.VMEM)
    hbm = pl.BlockSpec(memory_space=pl.ANY)
    smem = pl.BlockSpec(memory_space=pltpu.SMEM)
    out = jax.ShapeDtypeStruct((rows, cols), BF16)
    held = pltpu.VMEM((rows, cols), BF16)
    ext = 3 * rows
    width = cols // CHUNKS
    dma = pltpu.SemaphoreType.DMA
    grads = pl.pallas_call(
        functools.partial(body, n, cap, doc_lengths.shape[0]),
        out_shape=(held, held, held),
        in_specs=[hbm] * 5 + [smem] * 2,
        out_specs=(vmem, vmem, vmem),
        scratch_shapes=[
            pltpu.VMEM((rows, cols), BF16),
            pltpu.VMEM((rows, cols), BF16),
            pltpu.VMEM((blocks, LINKS), jnp.int32),
            pltpu.VMEM((8, 128), jnp.int32),
            dma((5,)),
            pltpu.VMEM((ext, cols), BF16),
            pltpu.VMEM((ext, cols), BF16),
            pltpu.VMEM((n, 8, 128), jnp.int32),
            pltpu.VMEM((n, 8, 128), F32),
            pltpu.VMEM((n * cap, rows), BF16),
            pltpu.VMEM((n * cap, 128), BF16),
            pltpu.VMEM((CHUNKS, n * cap, 2 * width), BF16),
            pltpu.VMEM((CHUNKS, n * cap, 2 * width), BF16),
            pltpu.VMEM((128, cols), BF16),
            pltpu.VMEM((128, cols), BF16),
            pltpu.VMEM((ext, cols), F32),
            pltpu.VMEM((ext, cols), F32),
            pltpu.VMEM((128, cols), F32),
            pltpu.VMEM((128, cols), F32),
            pltpu.VMEM((CHUNKS, n * cap, 2 * width), BF16),
            pltpu.VMEM((CHUNKS, n * cap, 2 * width), BF16),
            pltpu.VMEM((CHUNKS, RIM, 2 * width), BF16),
            pltpu.VMEM((CHUNKS, RIM, 2 * width), BF16),
            pltpu.VMEM((CHUNKS, rows, 2 * width), BF16),
            pltpu.VMEM((CHUNKS, rows, 2 * width), BF16),
            pltpu.VMEM((rows // BLK, BLK, WIN + 128), F32),
            dma((n,)), dma((n,)),
            dma((4 * CHUNKS,)), dma((4 * CHUNKS,)), dma((2 * CHUNKS,)), dma((2 * CHUNKS,)),
            dma((CHUNKS, n)), dma((CHUNKS, n)), dma((CHUNKS, n)), dma((CHUNKS, n)),
            dma((CHUNKS,)), dma((CHUNKS,)), dma((2 * CHUNKS,)), dma((2 * CHUNKS,)),
        ],
        compiler_params=pltpu.CompilerParams(
            collective_id=0, has_side_effects=True, vmem_limit_bytes=58 << 20
        ),
    )(queries, keys, values, grad_out, anchor_ids, link_counts, doc_lengths)
    return pl.pallas_call(
        emit,
        out_shape=(out, out, out),
        in_specs=[hbm] * 3,
        out_specs=(hbm, hbm, hbm),
        scratch_shapes=[dma((3,))],
        compiler_params=pltpu.CompilerParams(vmem_limit_bytes=1 << 20),
    )(*grads)


def solution(mesh):
    return jax.shard_map(
        on_device,
        mesh=mesh,
        in_specs=(
            P("seq", "head"),
            P("seq", "head"),
            P("seq", "head"),
            P("seq", "head"),
            P("seq", None),
            P("seq"),
            P(),
        ),
        out_specs=(P("seq", "head"), P("seq", "head"), P("seq", "head")),
        check_vma=False,
    )
```

```python
import functools

import jax
import jax.numpy as jnp
from jax import lax
from jax.experimental import pallas as pl
from jax.experimental.pallas import tpu as pltpu
from jax.sharding import PartitionSpec as P

HD = 128
BLK = 128
LINKS = 32
RIM = 2 * BLK
CHUNKS = 4
WIN = 5 * BLK
MESH = pl.DeviceIdType.MESH
F32 = jnp.float32
BF16 = jnp.bfloat16


def dot(a, b, ca, cb):
    return lax.dot_general(a, b, (((ca,), (cb,)), ((), ())), preferred_element_type=F32)


def body(
    n, cap, ndocs,
    q_hbm, k_ref, v_ref, go_hbm, ids_hbm, cnt_ref, len_ref,
    gq_ref, gk_ref, gv_ref,
    q_ref, go_ref, ids_s, meta_ref, l_ss,
    kx, vx, meta_all, rank_s, sel, own_hot, sendbuf, arr, pair_out, pair_in, ak, av,
    acck, accv, anck, ancv, slot_g, gsend, ginc, far_out, far_in, near_out, near_in, bias_s,
    meta_ss, meta_rs, m_ss, m_rs, r_ss, r_rs, a_ss, a_rs, g_ss, g_rs, p_ss, p_rs, f_ss, f_rs, b_ss, b_rs,
):
    rows, cols = q_hbm.shape
    heads = cols // HD
    blocks = rows // BLK
    chunks = CHUNKS
    width = cols // chunks
    scale = float(HD) ** (-0.5)
    me = lax.axis_index("seq")
    unroll = n <= 8

    def loop(lo, hi, f):
        def g(i, c):
            f(i)
            return c
        lax.fori_loop(lo, hi, g, 0, unroll=unroll)

    def peer(i):
        return lax.rem(me + i, n)

    def level(i):
        return lax.rem(me // 2 + i, n // 2)

    def at2(ref, z):
        return ref.at[pl.ds(pl.multiple_of(z * 2 * cap, 2 * cap), 2 * cap)]

    def at(ref, d):
        return ref.at[pl.ds(pl.multiple_of(d * cap, cap), cap)]

    def rcopy(src, dst, ss, rs, d):
        return pltpu.make_async_remote_copy(
            src_ref=src, dst_ref=dst, send_sem=ss, recv_sem=rs,
            device_id={"seq": d}, device_id_type=MESH,
        )

    barrier = pltpu.get_barrier_semaphore()
    loop(1, n, lambda i: pl.semaphore_signal(
        barrier, inc=1, device_id={"seq": peer(i)}, device_id_type=MESH))

    home = [
        pltpu.make_async_copy(src, dst, l_ss.at[i])
        for i, (src, dst) in enumerate((
            (ids_hbm, ids_s),
            (k_ref, kx.at[pl.ds(rows, rows)]),
            (v_ref, vx.at[pl.ds(rows, rows)]),
            (q_hbm, q_ref),
            (go_hbm, go_ref),
        ))
    ]
    for copy in home:
        copy.start()

    lane_a = lax.broadcasted_iota(jnp.int32, (128, 128), 0)
    lane_b = lax.broadcasted_iota(jnp.int32, (128, 128), 1)
    upper = (lane_a < lane_b).astype(BF16)
    home[0].wait()
    slot_lane = lax.broadcasted_iota(jnp.int32, (8, 128), 1)
    ids = jnp.full((8, 128), -1, jnp.int32)
    for b in range(blocks):
        listed = jnp.concatenate(
            [ids_s[b:b + 1], jnp.full((1, 128 - LINKS), -1, jnp.int32)], axis=1)
        moved = pltpu.roll(jnp.broadcast_to(listed, (8, 128)), b * LINKS, 1) if b else jnp.broadcast_to(listed, (8, 128))
        first_lane = b * LINKS
        ids = jnp.where((slot_lane >= first_lane) & (slot_lane < first_lane + cnt_ref[b]), moved, ids)
    meta_ref[...] = ids
    slot = lax.broadcasted_iota(jnp.int32, (cap, 128), 0)

    def hot(inside, rank):
        return jnp.where(
            (rank[0:1].astype(jnp.int32) == slot) & (inside[0:1] > 0.5), 1.0, 0.0
        ).astype(BF16)

    def inside_of(values, owner):
        return jnp.where((values >= owner * rows) & (values < (owner + 1) * rows), 1.0, 0.0)

    pl.semaphore_wait(barrier, n - 1)

    loop(1, n, lambda i: rcopy(
        meta_ref, meta_all.at[me], meta_ss.at[peer(i)], meta_rs.at[me], peer(i)).start())

    par = lax.rem(me, 2)
    mate = me + 1 - 2 * par

    def span(start, length):
        return pl.ds(pl.multiple_of(start, BLK), length)

    def pick(even, odd):
        return even + par * (odd - even)

    def chunk_cols(c):
        return pl.ds(c * width, width)

    kv = ((k_ref, kx), (v_ref, vx))

    def to_mate(c, part):
        start = pick(0, BLK) if part == 0 else pick(RIM, 0)
        length = RIM if part == 0 else BLK
        goal = pick(0, 2 * rows) + start
        return [
            rcopy(src.at[span(start, length), chunk_cols(c)],
                  dst.at[span(goal, length), chunk_cols(c)],
                  m_ss.at[4 * c + 2 * part + t], m_rs.at[4 * c + 2 * part + t], mate)
            for t, (src, dst) in enumerate(kv)
        ]

    ahead = jnp.clip(pick(me + 2, me - 2), 0, n - 1)
    behind = jnp.clip(pick(me - 2, me + 2), 0, n - 1)
    has_ahead = (pick(me + 2, me - 2) >= 0) & (pick(me + 2, me - 2) < n)
    has_behind = (pick(me - 2, me + 2) >= 0) & (pick(me - 2, me + 2) < n)

    def relay(c):
        return [
            rcopy(x.at[span(pick(2 * rows + BLK, 0), RIM), chunk_cols(c)],
                  x.at[span(pick(BLK, 2 * rows), RIM), chunk_cols(c)],
                  r_ss.at[2 * c + t], r_rs.at[2 * c + t], ahead)
            for t, x in enumerate((kx, vx))
        ]

    for c in range(chunks):
        for copy in to_mate(c, 0):
            copy.start()

    meta_all[me] = ids

    @pl.when(jnp.logical_not(has_behind))
    def _():
        kx[span(pick(BLK, 2 * rows), RIM)] = jnp.zeros((RIM, cols), BF16)
        vx[span(pick(BLK, 2 * rows), RIM)] = jnp.zeros((RIM, cols), BF16)

    acck[...] = jnp.zeros_like(acck)
    accv[...] = jnp.zeros_like(accv)
    for c in range(chunks):
        slot_g[c, blocks * LINKS:128] = jnp.zeros((128 - blocks * LINKS, 2 * width), BF16)
        slot_g[c, 128 + blocks * LINKS:] = jnp.zeros((128 - blocks * LINKS, 2 * width), BF16)
    ak[blocks * LINKS:] = jnp.zeros((128 - blocks * LINKS, cols), BF16)
    av[blocks * LINKS:] = jnp.zeros((128 - blocks * LINKS, cols), BF16)
    anck[...] = jnp.zeros_like(anck)
    ancv[...] = jnp.zeros_like(ancv)

    base = me * rows - RIM
    pos_l = base + lax.broadcasted_iota(jnp.int32, (8, rows + 2 * RIM), 1)
    pos_s = me * rows + lax.broadcasted_iota(jnp.int32, (rows, 128), 0)

    def count(k, c):
        start, dl, ds = c
        return (
            start + len_ref[k],
            dl + jnp.where(start <= pos_l, 1, 0),
            ds + jnp.where(start <= pos_s, 1, 0),
        )

    _, doc_l, doc_s = lax.fori_loop(
        0, ndocs, count,
        (jnp.int32(0), jnp.full(pos_l.shape, -1, jnp.int32), jnp.full(pos_s.shape, -1, jnp.int32)),
        unroll=ndocs <= 8,
    )
    doc_l = jnp.where((pos_l >= 0) & (pos_l < n * rows), doc_l, -1)

    def meta_wait(i):
        s = peer(i)
        rcopy(meta_ref, meta_all.at[s], meta_ss.at[s], meta_rs.at[s], s).wait()

    loop(1, n, meta_wait)
    row_id = me * rows + lax.broadcasted_iota(jnp.int32, (rows, 128), 0)
    every = meta_all[...].reshape(n * 8, 128)
    rank_s[...] = dot(inside_of(every, me).astype(BF16), upper, 1, 0).reshape(n, 8, 128)

    def sel_one(d):
        theirs = meta_all[d]
        oh = hot(inside_of(theirs, me), rank_s[d])
        place = jnp.where(theirs[0:1] == row_id, 1.0, 0.0).astype(BF16)
        at(sel, d)[...] = dot(oh, place, 1, 1).astype(BF16)

    loop(0, n, sel_one)

    floor = me // 2

    def a_copy(c, z, slot_of):
        return rcopy(at2(sendbuf.at[c], z), at2(arr.at[c], slot_of),
                     a_ss.at[c, z], a_rs.at[c, slot_of], 2 * z + par)

    for copy in home[1:]:
        copy.wait()
    for c in range(chunks):
        cs = slice(c * width, (c + 1) * width)
        sendbuf[c, :, :width] = dot(sel[...], kx[rows:2 * rows, cs], 1, 0).astype(BF16)
        sendbuf[c, :, width:] = dot(sel[...], vx[rows:2 * rows, cs], 1, 0).astype(BF16)
        at2(arr.at[c], floor)[...] = at2(sendbuf.at[c], floor)[...]
    for c in range(chunks):
        for copy in to_mate(c, 0):
            copy.wait()

        @pl.when(has_ahead)
        def _():
            for copy in relay(c):
                copy.start()

        loop(1, n // 2, lambda i: a_copy(c, level(i), floor).start())
        for copy in to_mate(c, 1):
            copy.start()

    for t in range(2):
        asked = meta_all[2 * floor + t]

        def own_one(z):
            inside = inside_of(asked, 2 * z + par)
            one = hot(inside, dot(inside.astype(BF16), upper, 1, 0))
            at(own_hot, 2 * z + t)[:, t * 128:(t + 1) * 128] = one
            at(own_hot, 2 * z + t)[:, (1 - t) * 128:(2 - t) * 128] = jnp.zeros_like(one)

        loop(0, n // 2, own_one)

    lanes = lax.broadcasted_iota(jnp.int32, (BLK, 128), 1)
    live = jnp.broadcast_to(ids[0:1], (BLK, 128)) >= 0
    for b in range(blocks):
        r0 = b * BLK
        same = doc_s[r0:r0 + BLK, 0:1] == doc_l[0:1, r0:r0 + WIN]
        linked = live & (lanes >= b * LINKS) & (lanes < (b + 1) * LINKS)
        bias_s[b] = jnp.concatenate(
            [jnp.where(same, 0.0, -1e30), jnp.where(linked, 0.0, -1e30)], axis=1)

    first = rows - RIM

    def far_copy(c):
        return rcopy(far_out.at[c], far_in.at[c], f_ss.at[c], f_rs.at[c], behind)

    def near_copy(c, part):
        length = BLK if part == 0 else RIM
        start = pick(0, RIM) if part == 0 else pick(BLK, 0)
        return rcopy(near_out.at[c, span(start, length)], near_in.at[c, span(start, length)],
                     b_ss.at[2 * c + part], b_rs.at[2 * c + part], mate)

    def g_copy(c, z, slot_of):
        return rcopy(at2(gsend.at[c], z), at2(ginc.at[c], slot_of),
                     g_ss.at[c, z], g_rs.at[c, slot_of], 2 * z + par)

    slots = blocks * LINKS

    def slots_of(t):
        return span(t * 128, slots)

    def pair_copy(c):
        return rcopy(pair_out.at[c, slots_of(1 - par)], pair_in.at[c, pl.ds(0, slots)],
                     p_ss.at[c], p_rs.at[c], mate)

    def back_copy(c):
        return rcopy(slot_g.at[c, slots_of(par)], slot_g.at[c, slots_of(par)],
                     p_ss.at[chunks + c], p_rs.at[chunks + c], mate)

    def merge(c):
        loop(1, n // 2, lambda i: a_copy(c, level(i), level(i)).wait())
        pair_out[c] = dot(own_hot[...], arr[c], 0, 0).astype(BF16)
        pair_copy(c).start()

    merge(0)
    for c in range(chunks):
        cs = slice(c * width, (c + 1) * width)
        for copy in to_mate(c, 1):
            copy.wait()

        @pl.when(has_ahead)
        def _():
            for copy in relay(c):
                copy.wait_send()

        @pl.when(has_behind)
        def _():
            for copy in relay(c):
                copy.wait_recv()

        pair_copy(c).wait()
        own = pair_out[c, span(par * 128, 128)]
        ak[:slots, cs] = own[:slots, :width] + pair_in[c, :, :width]
        av[:slots, cs] = own[:slots, width:] + pair_in[c, :, width:]
        for b in range(blocks):
            r0 = b * BLK
            w0 = first + r0

            def one_head(h, carry):
                col = pl.ds(pl.multiple_of(c * width + h * HD, HD), HD)
                qb = q_ref[r0:r0 + BLK, col]
                gb = go_ref[r0:r0 + BLK, col]
                kw = jnp.concatenate([kx[w0:w0 + WIN, col], ak[:, col]], axis=0)
                vw = jnp.concatenate([vx[w0:w0 + WIN, col], av[:, col]], axis=0)
                allowed = bias_s[b] == 0.0
                s = jnp.where(allowed, dot(qb, kw, 1, 1) * scale, -1e30)
                top = jnp.max(s, axis=1, keepdims=True)
                e = jnp.where(allowed, jnp.exp(s - top), 0.0)
                w = e / jnp.sum(e, axis=1, keepdims=True)
                wb = w.astype(BF16)
                gw = dot(gb, vw, 1, 1)
                delta = jnp.sum(wb.astype(F32) * gw, axis=1, keepdims=True)
                ds = (w * (gw - delta)).astype(BF16)
                gq_ref[r0:r0 + BLK, col] = (dot(ds, kw, 1, 0) * scale).astype(BF16)
                dk = dot(ds, qb, 0, 0) * scale
                dv = dot(wb, gb, 0, 0)
                acck[w0:w0 + WIN, col] += dk[:WIN]
                accv[w0:w0 + WIN, col] += dv[:WIN]
                anck[:, col] += dk[WIN:]
                ancv[:, col] += dv[WIN:]
                return carry

            lax.fori_loop(0, width // HD, one_head, 0, unroll=True)

        far = span(pick(BLK, 2 * rows), RIM)
        far_out[c, :, :width] = acck[far, cs].astype(BF16)
        far_out[c, :, width:] = accv[far, cs].astype(BF16)
        near = span(pick(2 * rows, RIM), BLK)
        near_out[c, span(pick(0, RIM), BLK), :width] = acck[near, cs].astype(BF16)
        near_out[c, span(pick(0, RIM), BLK), width:] = accv[near, cs].astype(BF16)

        @pl.when(has_behind)
        def _():
            far_copy(c).start()

        near_copy(c, 0).start()
        slot_g[c, span(par * 128, 128), :width] = anck[:, cs].astype(BF16)
        slot_g[c, span(par * 128, 128), width:] = ancv[:, cs].astype(BF16)
        back_copy(c).start()
        if c + 1 < chunks:
            merge(c + 1)
        back_copy(c).wait()
        gsend[c] = dot(own_hot[...], slot_g[c], 1, 0).astype(BF16)
        loop(1, n // 2, lambda i: g_copy(c, level(i), floor).start())
        at2(ginc.at[c], floor)[...] = at2(gsend.at[c], floor)[...]

    for c in range(chunks):
        cs = slice(c * width, (c + 1) * width)
        mine = span(pick(2 * rows + BLK, 0), RIM)

        @pl.when(has_behind)
        def _():
            far_copy(c).wait_send()

        @pl.when(has_ahead)
        def _():
            far_copy(c).wait_recv()
            acck[mine, cs] += far_in[c, :, :width].astype(F32)
            accv[mine, cs] += far_in[c, :, width:].astype(F32)

        near_out[c, span(pick(BLK, 0), RIM), :width] = acck[mine, cs].astype(BF16)
        near_out[c, span(pick(BLK, 0), RIM), width:] = accv[mine, cs].astype(BF16)
        near_copy(c, 1).start()

    for c in range(chunks):
        cs = slice(c * width, (c + 1) * width)
        loop(1, n // 2, lambda i: g_copy(c, level(i), level(i)).wait())
        acck[rows:2 * rows, cs] += dot(sel[...], ginc[c, :, :width], 0, 0)
        accv[rows:2 * rows, cs] += dot(sel[...], ginc[c, :, width:], 0, 0)

    for c in range(chunks):
        cs = slice(c * width, (c + 1) * width)
        for part in range(2):
            near_copy(c, part).wait_send()
            near_copy(c, part).wait_recv()
        gk_ref[:, cs] = (acck[rows:2 * rows, cs] + near_in[c, :, :width].astype(F32)).astype(BF16)
        gv_ref[:, cs] = (accv[rows:2 * rows, cs] + near_in[c, :, width:].astype(F32)).astype(BF16)


def emit(gq, gk, gv, oq, ok, ov, sems):
    copies = [
        pltpu.make_async_copy(src, dst, sems.at[i])
        for i, (src, dst) in enumerate(((gq, oq), (gk, ok), (gv, ov)))
    ]
    for copy in copies:
        copy.start()
    for copy in copies:
        copy.wait()


def on_device(queries, keys, values, grad_out, anchor_ids, link_counts, doc_lengths):
    rows, cols = queries.shape
    blocks = rows // BLK
    n = lax.axis_size("seq")
    cap = -(-(4 * blocks * LINKS // n) // 16) * 16
    vmem = pl.BlockSpec(memory_space=pltpu.VMEM)
    hbm = pl.BlockSpec(memory_space=pl.ANY)
    smem = pl.BlockSpec(memory_space=pltpu.SMEM)
    out = jax.ShapeDtypeStruct((rows, cols), BF16)
    held = pltpu.VMEM((rows, cols), BF16)
    ext = 3 * rows
    width = cols // CHUNKS
    dma = pltpu.SemaphoreType.DMA
    grads = pl.pallas_call(
        functools.partial(body, n, cap, doc_lengths.shape[0]),
        out_shape=(held, held, held),
        in_specs=[hbm] * 5 + [smem] * 2,
        out_specs=(vmem, vmem, vmem),
        scratch_shapes=[
            pltpu.VMEM((rows, cols), BF16),
            pltpu.VMEM((rows, cols), BF16),
            pltpu.VMEM((blocks, LINKS), jnp.int32),
            pltpu.VMEM((8, 128), jnp.int32),
            dma((5,)),
            pltpu.VMEM((ext, cols), BF16),
            pltpu.VMEM((ext, cols), BF16),
            pltpu.VMEM((n, 8, 128), jnp.int32),
            pltpu.VMEM((n, 8, 128), F32),
            pltpu.VMEM((n * cap, rows), BF16),
            pltpu.VMEM((n * cap, 256), BF16),
            pltpu.VMEM((CHUNKS, n * cap, 2 * width), BF16),
            pltpu.VMEM((CHUNKS, n * cap, 2 * width), BF16),
            pltpu.VMEM((CHUNKS, 256, 2 * width), BF16),
            pltpu.VMEM((CHUNKS, blocks * LINKS, 2 * width), BF16),
            pltpu.VMEM((128, cols), BF16),
            pltpu.VMEM((128, cols), BF16),
            pltpu.VMEM((ext, cols), F32),
            pltpu.VMEM((ext, cols), F32),
            pltpu.VMEM((128, cols), F32),
            pltpu.VMEM((128, cols), F32),
            pltpu.VMEM((CHUNKS, 256, 2 * width), BF16),
            pltpu.VMEM((CHUNKS, n * cap, 2 * width), BF16),
            pltpu.VMEM((CHUNKS, n * cap, 2 * width), BF16),
            pltpu.VMEM((CHUNKS, RIM, 2 * width), BF16),
            pltpu.VMEM((CHUNKS, RIM, 2 * width), BF16),
            pltpu.VMEM((CHUNKS, rows, 2 * width), BF16),
            pltpu.VMEM((CHUNKS, rows, 2 * width), BF16),
            pltpu.VMEM((rows // BLK, BLK, WIN + 128), F32),
            dma((n,)), dma((n,)),
            dma((4 * CHUNKS,)), dma((4 * CHUNKS,)), dma((2 * CHUNKS,)), dma((2 * CHUNKS,)),
            dma((CHUNKS, n // 2)), dma((CHUNKS, n // 2)), dma((CHUNKS, n // 2)), dma((CHUNKS, n // 2)),
            dma((2 * CHUNKS,)), dma((2 * CHUNKS,)),
            dma((CHUNKS,)), dma((CHUNKS,)), dma((2 * CHUNKS,)), dma((2 * CHUNKS,)),
        ],
        compiler_params=pltpu.CompilerParams(
            collective_id=0, has_side_effects=True, vmem_limit_bytes=58 << 20
        ),
    )(queries, keys, values, grad_out, anchor_ids, link_counts, doc_lengths)
    return pl.pallas_call(
        emit,
        out_shape=(out, out, out),
        in_specs=[hbm] * 3,
        out_specs=(hbm, hbm, hbm),
        scratch_shapes=[dma((3,))],
        compiler_params=pltpu.CompilerParams(vmem_limit_bytes=1 << 20),
    )(*grads)


def solution(mesh):
    return jax.shard_map(
        on_device,
        mesh=mesh,
        in_specs=(
            P("seq", "head"),
            P("seq", "head"),
            P("seq", "head"),
            P("seq", "head"),
            P("seq", None),
            P("seq"),
            P(),
        ),
        out_specs=(P("seq", "head"), P("seq", "head"), P("seq", "head")),
        check_vma=False,
    )
```

```python
import functools

import jax
import jax.numpy as jnp
from jax import lax
from jax.experimental import pallas as pl
from jax.experimental.pallas import tpu as pltpu
from jax.sharding import PartitionSpec as P

HD = 128
BLK = 128
LINKS = 32
RIM = 2 * BLK
CHUNKS = 4
WIN = 5 * BLK
MESH = pl.DeviceIdType.MESH
F32 = jnp.float32
BF16 = jnp.bfloat16


def dot(a, b, ca, cb):
    return lax.dot_general(a, b, (((ca,), (cb,)), ((), ())), preferred_element_type=F32)


def body(
    n, cap, ndocs,
    q_hbm, k_ref, v_ref, go_hbm, ids_hbm, cnt_ref, len_ref,
    gq_ref, gk_ref, gv_ref,
    q_ref, go_ref, ids_s, l_ss,
    kx, vx, meta_all, rank_s, sel, own_hot, sendbuf, arr, ak, av,
    acck, accv, anck, ancv, gsend, ginc, far_out, far_in, near_out, near_in, bias_s,
    meta_ss, meta_rs, m_ss, m_rs, r_ss, r_rs, a_ss, a_rs, g_ss, g_rs, f_ss, f_rs, b_ss, b_rs, pair_s,
):
    rows, cols = q_hbm.shape
    heads = cols // HD
    blocks = rows // BLK
    chunks = CHUNKS
    width = cols // chunks
    scale = float(HD) ** (-0.5)
    me = lax.axis_index("seq")
    unroll = n <= 8

    def loop(lo, hi, f):
        def g(i, c):
            f(i)
            return c
        lax.fori_loop(lo, hi, g, 0, unroll=unroll)

    def peer(i):
        return lax.rem(me + i, n)

    def at(ref, d):
        return ref.at[pl.ds(pl.multiple_of(d * cap, cap), cap)]

    def rcopy(src, dst, ss, rs, d):
        return pltpu.make_async_remote_copy(
            src_ref=src, dst_ref=dst, send_sem=ss, recv_sem=rs,
            device_id={"seq": d}, device_id_type=MESH,
        )

    par = lax.rem(me, 2)
    mate = me + 1 - 2 * par
    barrier = pltpu.get_barrier_semaphore()

    def greet(sem, d):
        pl.semaphore_signal(sem, inc=1, device_id={"seq": d}, device_id_type=MESH)

    @pl.when(par == 1)
    def _():
        greet(barrier, mate)

    loop(1, n // 2, lambda i: greet(barrier, 2 * lax.rem(me // 2 + i, n // 2) + 1))

    home = [
        pltpu.make_async_copy(src, dst, l_ss.at[i])
        for i, (src, dst) in enumerate((
            (ids_hbm, ids_s),
            (k_ref, kx.at[pl.ds(rows, rows)]),
            (v_ref, vx.at[pl.ds(rows, rows)]),
            (q_hbm, q_ref),
            (go_hbm, go_ref),
        ))
    ]
    for copy in home:
        copy.start()

    lane_a = lax.broadcasted_iota(jnp.int32, (128, 128), 0)
    lane_b = lax.broadcasted_iota(jnp.int32, (128, 128), 1)
    upper = (lane_a < lane_b).astype(BF16)
    home[0].wait()
    slot_lane = lax.broadcasted_iota(jnp.int32, (8, 128), 1)
    ids = jnp.full((8, 128), -1, jnp.int32)
    for b in range(blocks):
        listed = jnp.concatenate(
            [ids_s[b:b + 1], jnp.full((1, 128 - LINKS), -1, jnp.int32)], axis=1)
        moved = pltpu.roll(jnp.broadcast_to(listed, (8, 128)), b * LINKS, 1) if b else jnp.broadcast_to(listed, (8, 128))
        first_lane = b * LINKS
        ids = jnp.where((slot_lane >= first_lane) & (slot_lane < first_lane + cnt_ref[b]), moved, ids)
    meta_all[me] = ids

    @pl.when(par == 0)
    def _():
        pl.semaphore_wait(barrier, 1)
        greet(pair_s.at[0], mate)

    @pl.when(par == 1)
    def _():
        pl.semaphore_wait(pair_s.at[0], 1)

    def span(start, length):
        return pl.ds(pl.multiple_of(start, BLK), length)

    def pick(even, odd):
        return even + par * (odd - even)

    def chunk_cols(c):
        return pl.ds(c * width, width)

    kv = ((k_ref, kx), (v_ref, vx))

    def to_mate(c, part):
        start = pick(0, BLK) if part == 0 else pick(RIM, 0)
        length = RIM if part == 0 else BLK
        goal = pick(0, 2 * rows) + start
        return [
            rcopy(src.at[span(start, length), chunk_cols(c)],
                  dst.at[span(goal, length), chunk_cols(c)],
                  m_ss.at[4 * c + 2 * part + t], m_rs.at[4 * c + 2 * part + t], mate)
            for t, (src, dst) in enumerate(kv)
        ]

    floor = me // 2

    def meta_mate():
        return rcopy(meta_all.at[me], meta_all.at[me], meta_ss.at[mate], meta_rs.at[me], mate)

    def meta_level(z, slot_of):
        pair = meta_all.at[pl.ds(2 * floor, 2)]
        return rcopy(pair, pair, meta_ss.at[2 * z + par], meta_rs.at[2 * slot_of + par], 2 * z + par)

    def level(i):
        return lax.rem(floor + i, n // 2)

    meta_mate().start()
    for c in range(chunks):
        for copy in to_mate(c, 0):
            copy.start()

    slot = lax.broadcasted_iota(jnp.int32, (cap, 128), 0)

    def hot(inside, rank):
        return jnp.where(
            (rank[0:1].astype(jnp.int32) == slot) & (inside[0:1] > 0.5), 1.0, 0.0
        ).astype(BF16)

    def inside_of(values, owner):
        return jnp.where((values >= owner * rows) & (values < (owner + 1) * rows), 1.0, 0.0)

    ahead = jnp.clip(pick(me + 2, me - 2), 0, n - 1)
    behind = jnp.clip(pick(me - 2, me + 2), 0, n - 1)
    has_ahead = (pick(me + 2, me - 2) >= 0) & (pick(me + 2, me - 2) < n)
    has_behind = (pick(me - 2, me + 2) >= 0) & (pick(me - 2, me + 2) < n)

    def relay(c):
        return [
            rcopy(x.at[span(pick(2 * rows + BLK, 0), RIM), chunk_cols(c)],
                  x.at[span(pick(BLK, 2 * rows), RIM), chunk_cols(c)],
                  r_ss.at[2 * c + t], r_rs.at[2 * c + t], ahead)
            for t, x in enumerate((kx, vx))
        ]

    @pl.when(par == 1)
    def _():
        pl.semaphore_wait(barrier, n - 2)
        greet(pair_s.at[1], mate)

    @pl.when(par == 0)
    def _():
        pl.semaphore_wait(pair_s.at[1], 1)

    rcopy(meta_all.at[me], meta_all.at[mate], meta_ss.at[mate], meta_rs.at[mate], mate).wait()
    loop(1, n // 2, lambda i: meta_level(level(i), floor).start())

    @pl.when(jnp.logical_not(has_behind))
    def _():
        kx[span(pick(BLK, 2 * rows), RIM)] = jnp.zeros((RIM, cols), BF16)
        vx[span(pick(BLK, 2 * rows), RIM)] = jnp.zeros((RIM, cols), BF16)

    acck[...] = jnp.zeros_like(acck)
    accv[...] = jnp.zeros_like(accv)
    anck[...] = jnp.zeros_like(anck)
    ancv[...] = jnp.zeros_like(ancv)

    def own_one(o):
        inside = inside_of(ids, o)
        at(own_hot, o)[...] = hot(inside, dot(inside.astype(BF16), upper, 1, 0))

    loop(0, n, own_one)

    base = me * rows - RIM
    pos_l = base + lax.broadcasted_iota(jnp.int32, (8, rows + 2 * RIM), 1)
    pos_s = me * rows + lax.broadcasted_iota(jnp.int32, (rows, 128), 0)

    def count(k, c):
        start, dl, ds = c
        return (
            start + len_ref[k],
            dl + jnp.where(start <= pos_l, 1, 0),
            ds + jnp.where(start <= pos_s, 1, 0),
        )

    _, doc_l, doc_s = lax.fori_loop(
        0, ndocs, count,
        (jnp.int32(0), jnp.full(pos_l.shape, -1, jnp.int32), jnp.full(pos_s.shape, -1, jnp.int32)),
        unroll=ndocs <= 8,
    )
    doc_l = jnp.where((pos_l >= 0) & (pos_l < n * rows), doc_l, -1)

    def hand_on(c):
        for copy in to_mate(c, 0):
            copy.wait()

        @pl.when(has_ahead)
        def _():
            for copy in relay(c):
                copy.start()

        for copy in to_mate(c, 1):
            copy.start()

    hand_on(0)
    loop(1, n // 2, lambda i: meta_level(level(i), level(i)).wait())
    row_id = me * rows + lax.broadcasted_iota(jnp.int32, (rows, 128), 0)
    every = meta_all[...].reshape(n * 8, 128)
    rank_s[...] = dot(inside_of(every, me).astype(BF16), upper, 1, 0).reshape(n, 8, 128)

    def sel_one(d):
        theirs = meta_all[d]
        oh = hot(inside_of(theirs, me), rank_s[d])
        place = jnp.where(theirs[0:1] == row_id, 1.0, 0.0).astype(BF16)
        at(sel, d)[...] = dot(oh, place, 1, 1).astype(BF16)

    loop(0, n, sel_one)
    def a_copy(c, d, slot_of):
        return rcopy(at(sendbuf.at[c], d), at(arr.at[c], slot_of),
                     a_ss.at[c, d], a_rs.at[c, slot_of], d)

    for copy in home[1:]:
        copy.wait()
    for c in range(chunks):
        cs = slice(c * width, (c + 1) * width)
        sendbuf[c, :, :width] = dot(sel[...], kx[rows:2 * rows, cs], 1, 0).astype(BF16)
        sendbuf[c, :, width:] = dot(sel[...], vx[rows:2 * rows, cs], 1, 0).astype(BF16)
        at(arr.at[c], me)[...] = at(sendbuf.at[c], me)[...]
    for c in range(chunks):
        if c:
            hand_on(c)
        loop(1, n, lambda i: a_copy(c, peer(i), me).start())

    lanes = lax.broadcasted_iota(jnp.int32, (BLK, 128), 1)
    live = jnp.broadcast_to(ids[0:1], (BLK, 128)) >= 0
    for b in range(blocks):
        r0 = b * BLK
        same = doc_s[r0:r0 + BLK, 0:1] == doc_l[0:1, r0:r0 + WIN]
        linked = live & (lanes >= b * LINKS) & (lanes < (b + 1) * LINKS)
        bias_s[b] = jnp.concatenate(
            [jnp.where(same, 0.0, -1e30), jnp.where(linked, 0.0, -1e30)], axis=1)

    first = rows - RIM

    def far_copy(c):
        return rcopy(far_out.at[c], far_in.at[c], f_ss.at[c], f_rs.at[c], behind)

    def near_copy(c, part):
        length = BLK if part == 0 else RIM
        start = pick(0, RIM) if part == 0 else pick(BLK, 0)
        return rcopy(near_out.at[c, span(start, length)], near_in.at[c, span(start, length)],
                     b_ss.at[2 * c + part], b_rs.at[2 * c + part], mate)

    def g_copy(c, d, slot_of):
        return rcopy(at(gsend.at[c], d), at(ginc.at[c], slot_of),
                     g_ss.at[c, d], g_rs.at[c, slot_of], d)

    mine = span(pick(2 * rows + BLK, 0), RIM)

    def finish(c):
        cs = slice(c * width, (c + 1) * width)

        @pl.when(has_behind)
        def _():
            far_copy(c).wait_send()

        @pl.when(has_ahead)
        def _():
            far_copy(c).wait_recv()
            acck[mine, cs] += far_in[c, :, :width].astype(F32)
            accv[mine, cs] += far_in[c, :, width:].astype(F32)

        near_out[c, span(pick(BLK, 0), RIM), :width] = acck[mine, cs].astype(BF16)
        near_out[c, span(pick(BLK, 0), RIM), width:] = accv[mine, cs].astype(BF16)
        near_copy(c, 1).start()

    def take(c):
        cs = slice(c * width, (c + 1) * width)
        loop(1, n, lambda i: g_copy(c, peer(i), peer(i)).wait())
        acck[rows:2 * rows, cs] += dot(sel[...], ginc[c, :, :width], 0, 0)
        accv[rows:2 * rows, cs] += dot(sel[...], ginc[c, :, width:], 0, 0)

    for c in range(chunks):
        cs = slice(c * width, (c + 1) * width)
        for copy in to_mate(c, 1):
            copy.wait()

        @pl.when(has_ahead)
        def _():
            for copy in relay(c):
                copy.wait_send()

        @pl.when(has_behind)
        def _():
            for copy in relay(c):
                copy.wait_recv()

        loop(1, n, lambda i: a_copy(c, peer(i), peer(i)).wait())
        got = dot(own_hot[...], arr[c], 0, 0).astype(BF16)
        ak[:, cs] = got[:, :width]
        av[:, cs] = got[:, width:]
        for b in range(blocks):
            r0 = b * BLK
            w0 = first + r0

            def one_head(h, carry):
                col = pl.ds(pl.multiple_of(c * width + h * HD, HD), HD)
                qb = q_ref[r0:r0 + BLK, col]
                gb = go_ref[r0:r0 + BLK, col]
                kw = jnp.concatenate([kx[w0:w0 + WIN, col], ak[:, col]], axis=0)
                vw = jnp.concatenate([vx[w0:w0 + WIN, col], av[:, col]], axis=0)
                allowed = bias_s[b] == 0.0
                s = jnp.where(allowed, dot(qb, kw, 1, 1) * scale, -1e30)
                top = jnp.max(s, axis=1, keepdims=True)
                e = jnp.where(allowed, jnp.exp(s - top), 0.0)
                w = e / jnp.sum(e, axis=1, keepdims=True)
                wb = w.astype(BF16)
                gw = dot(gb, vw, 1, 1)
                delta = jnp.sum(wb.astype(F32) * gw, axis=1, keepdims=True)
                ds = (w * (gw - delta)).astype(BF16)
                gq_ref[r0:r0 + BLK, col] = (dot(ds, kw, 1, 0) * scale).astype(BF16)
                dk = dot(ds, qb, 0, 0) * scale
                dv = dot(wb, gb, 0, 0)
                acck[w0:w0 + WIN, col] += dk[:WIN]
                accv[w0:w0 + WIN, col] += dv[:WIN]
                anck[:, col] += dk[WIN:]
                ancv[:, col] += dv[WIN:]
                return carry

            lax.fori_loop(0, width // HD, one_head, 0, unroll=True)

        far = span(pick(BLK, 2 * rows), RIM)
        far_out[c, :, :width] = acck[far, cs].astype(BF16)
        far_out[c, :, width:] = accv[far, cs].astype(BF16)
        near = span(pick(2 * rows, RIM), BLK)
        near_out[c, span(pick(0, RIM), BLK), :width] = acck[near, cs].astype(BF16)
        near_out[c, span(pick(0, RIM), BLK), width:] = accv[near, cs].astype(BF16)

        @pl.when(has_behind)
        def _():
            far_copy(c).start()

        near_copy(c, 0).start()
        gsend[c, :, :width] = dot(own_hot[...], anck[:, cs].astype(BF16), 1, 0).astype(BF16)
        gsend[c, :, width:] = dot(own_hot[...], ancv[:, cs].astype(BF16), 1, 0).astype(BF16)
        loop(1, n, lambda i: g_copy(c, peer(i), me).start())
        at(ginc.at[c], me)[...] = at(gsend.at[c], me)[...]
        if 1 <= c < chunks - 1:
            finish(c - 1)
        if c == chunks - 2:
            finish(c)

    for c in range(chunks - 1):
        take(c)
    finish(chunks - 1)
    take(chunks - 1)

    for c in range(chunks):
        cs = slice(c * width, (c + 1) * width)
        for part in range(2):
            near_copy(c, part).wait_send()
            near_copy(c, part).wait_recv()
        gk_ref[:, cs] = (acck[rows:2 * rows, cs] + near_in[c, :, :width].astype(F32)).astype(BF16)
        gv_ref[:, cs] = (accv[rows:2 * rows, cs] + near_in[c, :, width:].astype(F32)).astype(BF16)


def emit(gq, gk, gv, oq, ok, ov, sems):
    copies = [
        pltpu.make_async_copy(src, dst, sems.at[i])
        for i, (src, dst) in enumerate(((gq, oq), (gk, ok), (gv, ov)))
    ]
    for copy in copies:
        copy.start()
    for copy in copies:
        copy.wait()


def on_device(queries, keys, values, grad_out, anchor_ids, link_counts, doc_lengths):
    rows, cols = queries.shape
    blocks = rows // BLK
    n = lax.axis_size("seq")
    cap = -(-(4 * blocks * LINKS // n) // 16) * 16
    vmem = pl.BlockSpec(memory_space=pltpu.VMEM)
    hbm = pl.BlockSpec(memory_space=pl.ANY)
    smem = pl.BlockSpec(memory_space=pltpu.SMEM)
    out = jax.ShapeDtypeStruct((rows, cols), BF16)
    held = pltpu.VMEM((rows, cols), BF16)
    ext = 3 * rows
    width = cols // CHUNKS
    dma = pltpu.SemaphoreType.DMA
    grads = pl.pallas_call(
        functools.partial(body, n, cap, doc_lengths.shape[0]),
        out_shape=(held, held, held),
        in_specs=[hbm] * 5 + [smem] * 2,
        out_specs=(vmem, vmem, vmem),
        scratch_shapes=[
            pltpu.VMEM((rows, cols), BF16),
            pltpu.VMEM((rows, cols), BF16),
            pltpu.VMEM((blocks, LINKS), jnp.int32),
            dma((5,)),
            pltpu.VMEM((ext, cols), BF16),
            pltpu.VMEM((ext, cols), BF16),
            pltpu.VMEM((n, 8, 128), jnp.int32),
            pltpu.VMEM((n, 8, 128), F32),
            pltpu.VMEM((n * cap, rows), BF16),
            pltpu.VMEM((n * cap, 128), BF16),
            pltpu.VMEM((CHUNKS, n * cap, 2 * width), BF16),
            pltpu.VMEM((CHUNKS, n * cap, 2 * width), BF16),
            pltpu.VMEM((128, cols), BF16),
            pltpu.VMEM((128, cols), BF16),
            pltpu.VMEM((ext, cols), F32),
            pltpu.VMEM((ext, cols), F32),
            pltpu.VMEM((128, cols), F32),
            pltpu.VMEM((128, cols), F32),
            pltpu.VMEM((CHUNKS, n * cap, 2 * width), BF16),
            pltpu.VMEM((CHUNKS, n * cap, 2 * width), BF16),
            pltpu.VMEM((CHUNKS, RIM, 2 * width), BF16),
            pltpu.VMEM((CHUNKS, RIM, 2 * width), BF16),
            pltpu.VMEM((CHUNKS, rows, 2 * width), BF16),
            pltpu.VMEM((CHUNKS, rows, 2 * width), BF16),
            pltpu.VMEM((rows // BLK, BLK, WIN + 128), F32),
            dma((n,)), dma((n,)),
            dma((4 * CHUNKS,)), dma((4 * CHUNKS,)), dma((2 * CHUNKS,)), dma((2 * CHUNKS,)),
            dma((CHUNKS, n)), dma((CHUNKS, n)), dma((CHUNKS, n)), dma((CHUNKS, n)),
            dma((CHUNKS,)), dma((CHUNKS,)), dma((2 * CHUNKS,)), dma((2 * CHUNKS,)),
            pltpu.SemaphoreType.REGULAR((2,)),
        ],
        compiler_params=pltpu.CompilerParams(
            collective_id=0, has_side_effects=True, vmem_limit_bytes=58 << 20
        ),
    )(queries, keys, values, grad_out, anchor_ids, link_counts, doc_lengths)
    return pl.pallas_call(
        emit,
        out_shape=(out, out, out),
        in_specs=[hbm] * 3,
        out_specs=(hbm, hbm, hbm),
        scratch_shapes=[dma((3,))],
        compiler_params=pltpu.CompilerParams(vmem_limit_bytes=1 << 20),
    )(*grads)


def solution(mesh):
    return jax.shard_map(
        on_device,
        mesh=mesh,
        in_specs=(
            P("seq", "head"),
            P("seq", "head"),
            P("seq", "head"),
            P("seq", "head"),
            P("seq", None),
            P("seq"),
            P(),
        ),
        out_specs=(P("seq", "head"), P("seq", "head"), P("seq", "head")),
        check_vma=False,
    )
```
